512 devices in a mesh: sector: 64 (over x, z, core), mpo: 8 (over y).
Axes of the slice: x: 4, y: 8, z: 8, core: 2. Of those that a mesh axis runs over, the one named last changes fastest.
Arguments:
- wavefunction: bfloat16 [64, 512, 512], P('sector'), may hold values from -6 to 6
- env_left: bfloat16 [32, 64, 512, 512], P('mpo', 'sector'), may hold values from -0.25 to 0.25
- env_right: bfloat16 [32, 64, 512, 512], P('mpo', 'sector'), may hold values from -0.046875 to 0.046875
- row_len: int32 [64], P('sector'), may hold values from 1 to 512, 20480 in all
- col_len: int32 [64], P('sector'), may hold values from 1 to 512, 20480 in all
- charge_shift: int32 [32], P('mpo'), may hold values from -1 to 1
- present: int32 [32, 64], P('mpo', 'sector'), may hold values 0 or 1
Outputs:
- first_image: bfloat16 [64, 512, 512], P('sector', 'mpo')
- second_image: bfloat16 [64, 512, 512], P('sector', 'mpo')
The draws below stay inside these ranges and needn't reach their ends.
All inputs are finite; a program needn't handle non-finite values. No bound on the sum of `row_len` or of `col_len` or of `present` on one device may be relied on, other than what follows from the above.
Results may differ from the reference program's by a relative error of at most 0.0065.
Values may be sent and summed in bfloat16 or wider, within the bound.
A program may use at most 64 MiB of HBM per device.

```python
import math
import jax
import jax.numpy as jnp
import numpy as np
from jax import lax

B = 512
W = 32
Q = 64
N_SECTOR = 64


def plant(values, rng, smallest, top_value):
    place = [jax.random.randint(jax.random.fold_in(rng, axis), (), 0, length) for axis, length in enumerate(values.shape)]
    widest = values.shape.index(max(values.shape))
    neighbour = place[:widest] + [(place[widest] + 1) % values.shape[widest]] + place[widest + 1:]
    return values.at[tuple(place)].set(smallest).at[tuple(neighbour)].set(top_value)


def shard_levels(stream_key, shape, split, least, top_value):
    factor_of = 1.0
    for dim, shards_of in split:
        heights = jax.random.uniform(jax.random.fold_in(jax.random.fold_in(stream_key, 6), dim), (shards_of,), jnp.float32, least / len(split), top_value / len(split))
        factor_of = factor_of * jnp.repeat(jnp.exp(heights), shape[dim] // shards_of).reshape((-1,) + (1,) * (len(shape) - 1 - dim))
    return factor_of


def split_up(number_of, total, reach, slope):
    weights = [(1 << 20) // math.isqrt(grade ** slope) + 1 for grade in range(2, number_of + 1)]
    surplus, counts = total - reach - (number_of - 1), [1] * (number_of - 1)
    while surplus > 0:
        movable = [i for i in range(number_of - 1) if counts[i] < reach]
        whole, budget = sum([weights[i] for i in movable]), surplus
        for i in movable:
            extra = min(reach - counts[i], max(1, budget * weights[i] // whole), surplus)
            counts[i] = counts[i] + extra
            surplus = surplus - extra
    return np.array([reach] + counts)


def ragged_sizes(rng, amount, total, bound, lean):
    if amount == 2:
        one = jax.random.randint(rng, (), max(1, total - bound), min(bound, total - 1) + 1)
        return jnp.stack([one, total - one])
    tallies = jnp.asarray(split_up(amount, total, bound, lean), jnp.int32)
    twos = (amount - 1) // 2
    giver, taker = tallies[1:1 + 2 * twos:2], tallies[2:2 + 2 * twos:2]
    slack = jnp.minimum(giver - 1, bound - taker)
    passed = jax.random.randint(jax.random.fold_in(rng, 1), (twos,), 0, 1 << 20) % (slack + 1)
    tallies = tallies.at[1:1 + 2 * twos:2].set(giver - passed).at[2:2 + 2 * twos:2].set(taker + passed)
    return tallies[jax.random.permutation(jax.random.fold_in(rng, 2), amount)]


def scatter_about(key, extent, spread, limit, cuts=(), held_as=jnp.bfloat16):
    drawn = spread * jax.random.normal(key, extent, jnp.float32)
    if cuts:
        drawn = drawn * shard_levels(key, extent, cuts, -0.22, 0.18)
    return jnp.clip(drawn, -limit, limit).astype(held_as)


def setup_inputs(seed: int = 0) -> dict:
    arg_keys = jax.random.split(jax.random.key(seed), 8)
    wavefunction = scatter_about(arg_keys[0], (Q, B, B), 1.0, 6.0, ((0, 64),))
    env_left = scatter_about(arg_keys[1], (W, Q, B, B), B ** -0.5, 0.25, ((0, 8), (1, 64)))
    env_right = scatter_about(arg_keys[2], (W, Q, B, B), (B * W) ** -0.5, 0.046875, ((0, 8), (1, 64)))
    row_len = ragged_sizes(arg_keys[3], Q, Q * B * 5 // 8, B, 2).astype(jnp.int32)
    col_len = ragged_sizes(arg_keys[4], Q, Q * B * 5 // 8, B, 2).astype(jnp.int32)
    charge_shift = plant(jax.random.randint(arg_keys[5], (W,), -1, 2), jax.random.fold_in(arg_keys[5], 1), -1, 1).astype(jnp.int32)
    present = plant((jax.random.randint(arg_keys[6], (W, Q), 0, 4) < 3).astype(jnp.int32), jax.random.fold_in(arg_keys[6], 1), 0, 1)
    return dict(wavefunction=wavefunction, env_left=env_left, env_right=env_right, row_len=row_len, col_len=col_len, charge_shift=charge_shift, present=present)


epsilon = 1e-06

def length_masks(lengths):
    position = jnp.arange(B, dtype=jnp.int32)
    return (position[None, :] < lengths[:, None]).astype(jnp.float32)

def apply_operator(masked_wave, env_left, env_right, charge_shift, present):
    padded = jnp.pad(masked_wave, ((1, 1), (0, 0), (0, 0)))

    def one_term(accumulated, inputs):
        left_w, right_w, shift_w, present_w = inputs
        begin = (1 - shift_w).astype(jnp.int32)
        source = lax.dynamic_slice_in_dim(padded, begin, N_SECTOR, 0)
        inner_part = jnp.einsum('qij,qjk->qik', left_w.astype(jnp.float32), source.astype(jnp.float32))
        inner_part = (inner_part * present_w.astype(jnp.float32)[:, None, None]).astype(jnp.bfloat16)
        accumulated = accumulated + jnp.einsum('qij,qkj->qik', inner_part.astype(jnp.float32), right_w.astype(jnp.float32))
        return (accumulated, None)
    start_sum = jnp.zeros((N_SECTOR, B, B), jnp.float32)
    accumulated, unused = lax.scan(one_term, start_sum, (env_left, env_right, charge_shift, present))
    return accumulated

def reference(wavefunction, env_left, env_right, row_len, col_len, charge_shift, present):
    row_mask = length_masks(row_len)
    col_mask = length_masks(col_len)
    cell_mask = row_mask[:, :, None] * col_mask[:, None, :]
    masked_wave = (wavefunction * cell_mask).astype(jnp.bfloat16)
    first_image = apply_operator(masked_wave, env_left, env_right, charge_shift, present) * cell_mask
    mean_square = jnp.sum(first_image * first_image) / (N_SECTOR * B * B)
    basis_vector = (first_image * (1.0 / jnp.sqrt(mean_square + epsilon))).astype(jnp.bfloat16)
    second_image = apply_operator(basis_vector, env_left, env_right, charge_shift, present) * cell_mask
    return (first_image.astype(jnp.bfloat16), second_image.astype(jnp.bfloat16))
```

```python
import functools

import jax
import jax.numpy as jnp
from jax import lax
from jax.experimental import pallas as pl
from jax.experimental.pallas import tpu as pltpu
from jax.sharding import PartitionSpec as P

epsilon = 1e-06
MESH = pl.DeviceIdType.MESH
F32, BF16 = jnp.float32, jnp.bfloat16
CHUNKS = 4


def kernel(dims, wave, env_left, env_right, row_len, col_len, shift, present, out1, out2,
           raw, rmat, rtrans, lcat, u, own, rs_send, rs_recv, sq_send, sq_y, sq_z, sq_x, sq_c, obuf,
           ld, ss, rs, *fields):
    n, ns, nx, nz, wl, b = dims
    h = n // 2
    share = b // n
    crow = b // CHUNKS
    v1, v2 = fields[:CHUNKS], fields[CHUNKS:]

    s = lax.axis_index("sector")
    y = lax.axis_index("mpo")
    core = lax.rem(s, 2)
    z = lax.rem(s // 2, nz)
    x = s // (2 * nz)
    near_s = s + 1 - 2 * core
    far_s = lax.rem(s + ns + 2 * core - 1, ns)
    near, far = (near_s, y), (far_s, y)

    def ypeer(k):
        return (s, lax.rem(y + n + k, n))

    def zpeer(k):
        return ((x * nz + lax.rem(z + k, nz)) * 2 + core, y)

    def xpeer(k):
        return ((lax.rem(x + k, nx) * nz + z) * 2 + core, y)

    bar = pltpu.get_barrier_semaphore()
    partners = [ypeer(k) for k in range(1, n)] + [near, far]
    partners += [zpeer(k) for k in range(1, nz)] + [xpeer(k) for k in range(1, nx)]
    for p in partners:
        pl.semaphore_signal(bar, inc=1, device_id=p, device_id_type=MESH)

    load_wave = pltpu.make_async_copy(wave.at[0], raw, ld.at[0])
    load_wave.start()
    load_r, load_l = [], []
    for w in range(wl):
        c = pltpu.make_async_copy(env_right.at[w, 0], rmat.at[w], ld.at[1 + w])
        c.start()
        load_r.append(c)
    for w in range(wl):
        c = pltpu.make_async_copy(env_left.at[w, 0], lcat.at[:, w * b:(w + 1) * b], ld.at[1 + wl + w])
        c.start()
        load_l.append(c)

    rl, cl = row_len[0], col_len[0]
    near_shift = 2 * core - 1
    slot, weight = [], []
    for w in range(wl):
        sh = shift[w]
        source = s - sh
        slot.append(jnp.where(sh == 0, 0, jnp.where(sh == near_shift, 1, 2)))
        ok = jnp.logical_and(source >= 0, source < ns)
        weight.append(jnp.where(ok, present[w, 0], 0).astype(F32))

    sends = []
    counter = [0]
    sem_of = {}

    def sem(key):
        if key not in sem_of:
            sem_of[key] = counter[0]
            counter[0] += 1
        return sem_of[key]

    def send(src, dst, key, dev):
        i = sem(key)
        c = pltpu.make_async_remote_copy(src, dst, ss.at[i], rs.at[i], device_id=dev, device_id_type=MESH)
        c.start()
        sends.append(c)

    def arrived(dst, key):
        i = sem(key)
        pltpu.make_async_remote_copy(dst, dst, ss.at[i], rs.at[i], device_id=near, device_id_type=MESH).wait_recv()

    load_wave.wait()
    cmask = lax.broadcasted_iota(jnp.int32, (crow, b), 1) < cl
    rio = lax.broadcasted_iota(jnp.int32, (crow, b), 0)
    for c in range(CHUNKS):
        keep = jnp.logical_and(cmask, rio + c * crow < rl)
        v1[c][0] = jnp.where(keep, raw[c * crow:(c + 1) * crow, :].astype(F32), 0.0).astype(BF16)
    pl.semaphore_wait(bar, len(partners))
    for c in range(CHUNKS):
        send(v1[c].at[0], v1[c].at[2], ("h1f", c), far)
        send(v1[c].at[0], v1[c].at[1], ("h1n", c), near)

    for w in range(wl):
        load_r[w].wait()
        rtrans[w] = rmat[w].T
    for w in range(wl):
        load_l[w].wait()

    for c in range(CHUNKS):
        arrived(v1[c].at[1], ("h1n", c))
        arrived(v1[c].at[2], ("h1f", c))
        for w in range(wl):
            part = jnp.dot(v1[c][slot[w]], rtrans[w], preferred_element_type=F32)
            u[w * b + c * crow:w * b + (c + 1) * crow, :] = (part * weight[w]).astype(BF16)

    def start(k):
        return pl.multiple_of(lax.rem(y + n + k, n) * share, share)

    order = [h]
    for k in range(h - 1, 0, -1):
        order += [k, -k]
    order += [0]

    def reduce_scatter(app, between):
        for a in range(0, n, 2):
            k0, k1 = order[a], order[a + 1]
            lhs = jnp.concatenate([lcat[pl.ds(start(k0), share), :], lcat[pl.ds(start(k1), share), :]], axis=0)
            part = jnp.dot(lhs, u[...], preferred_element_type=F32)
            for k, block in ((k0, part[:share]), (k1, part[share:])):
                if k == 0:
                    own[...] = block
                else:
                    rs_send[app, k % n] = block.astype(BF16)
                    send(rs_send.at[app, k % n], rs_recv.at[app, k % n], ("rs", app, k), ypeer(k))
        between()
        total = own[...]
        for k in order[:-1]:
            arrived(rs_recv.at[app, k % n], ("rs", app, k))
            total = total + rs_recv[app, k % n].astype(F32)
        keep_r = lax.broadcasted_iota(jnp.int32, (share, b), 0) + y * share < rl
        keep_c = lax.broadcasted_iota(jnp.int32, (share, b), 1) < cl
        return jnp.where(jnp.logical_and(keep_r, keep_c), total, 0.0)

    image = reduce_scatter(0, lambda: None)

    def field(r, layer):
        if r in (0, h):
            return v2[0].at[layer, 0 if r == 0 else 1]
        return v2[abs(r)].at[layer, 0 if r > 0 else 1]

    v2[0][0, 0] = image.astype(BF16)
    square = image * image
    square = jnp.sum(square.reshape(share // 8, 8, b), axis=0)
    tile = square[:, 0:128]
    for q in range(128, b, 128):
        tile = tile + square[:, q:q + 128]
    sq_send[0] = tile

    def hand_on(r):
        send(field(r, 0), field(r, 2), ("h2f", r), far)
        send(field(r, 0), field(r, 1), ("h2n", r), near)

    near_first = []
    for k in range(1, h):
        near_first += [k, -k]
    near_first += [h]
    for k in near_first:
        send(field(0, 0), field(h if k == h else -k, 0), ("ag", h if k == h else -k), ypeer(k))
    hand_on(0)
    for k in range(1, n):
        send(sq_send.at[0], sq_y.at[k - 1], ("sqy", k), ypeer(k))
    write1 = pltpu.make_async_copy(v2[0].at[0, 0], out1.at[0], ld.at[0])
    write1.start()

    for r in near_first:
        arrived(field(r, 0), ("ag", r))
        hand_on(r)

    total = sq_send[0]
    for k in range(1, n):
        arrived(sq_y.at[k - 1], ("sqy", k))
        total = total + sq_y[k - 1]
    sq_send[1] = total
    for k in range(1, nz):
        send(sq_send.at[1], sq_z.at[k - 1], ("sqz", k), zpeer(k))

    for g in list(range(1, h)) + [0]:
        members = (g, -g) if g else (0, h)
        for r in members:
            arrived(field(r, 1), ("h2n", r))
            arrived(field(r, 2), ("h2f", r))
        for w in range(wl):
            lhs = v2[g][slot[w]].reshape(2 * share, b)
            part = (jnp.dot(lhs, rtrans[w], preferred_element_type=F32) * weight[w]).astype(BF16)
            for i, r in enumerate(members):
                u[pl.ds(w * b + start(r), share), :] = part[i * share:(i + 1) * share]

    def norm_steps():
        total = sq_send[1]
        for k in range(1, nz):
            arrived(sq_z.at[k - 1], ("sqz", k))
            total = total + sq_z[k - 1]
        sq_send[2] = total
        for k in range(1, nx):
            send(sq_send.at[2], sq_x.at[k - 1], ("sqx", k), xpeer(k))
        for k in range(1, nx):
            arrived(sq_x.at[k - 1], ("sqx", k))
            total = total + sq_x[k - 1]
        sq_send[3] = total
        send(sq_send.at[3], sq_c, ("sqc", 0), near)
        arrived(sq_c, ("sqc", 0))
        sq_send[4] = total + sq_c[...]

    second = reduce_scatter(1, norm_steps)
    norm = jnp.sum(sq_send[4]) / (ns * b * b) + epsilon
    obuf[...] = (second * (1.0 / jnp.sqrt(jnp.full((1, 1), norm, F32)))).astype(BF16)
    write2 = pltpu.make_async_copy(obuf, out2.at[0], ld.at[1])
    write2.start()
    for c in sends:
        c.wait_send()
    write1.wait()
    write2.wait()
    assert counter[0] <= ss.shape[0]


def shards(dims, wavefunction, env_left, env_right, row_len, col_len, charge_shift, present):
    n, ns, nx, nz, wl, b = dims
    share, crow = b // n, b // CHUNKS
    any_spec = pl.BlockSpec(memory_space=pl.ANY)
    smem = pl.BlockSpec(memory_space=pltpu.SMEM)
    out = jax.ShapeDtypeStruct((1, share, b), BF16)
    sems = 2 * CHUNKS + 2 * (n - 1) + (n - 1) + 2 * n + (n - 1) + (nz - 1) + (nx - 1) + 1
    scratch = [
        pltpu.VMEM((b, b), BF16),
        pltpu.VMEM((wl, b, b), BF16),
        pltpu.VMEM((wl, b, b), BF16),
        pltpu.VMEM((b, wl * b), BF16),
        pltpu.VMEM((wl * b, b), BF16),
        pltpu.VMEM((share, b), F32),
        pltpu.VMEM((2, n, share, b), BF16),
        pltpu.VMEM((2, n, share, b), BF16),
        pltpu.VMEM((5, 8, 128), F32),
        pltpu.VMEM((n - 1, 8, 128), F32),
        pltpu.VMEM((max(nz - 1, 1), 8, 128), F32),
        pltpu.VMEM((max(nx - 1, 1), 8, 128), F32),
        pltpu.VMEM((8, 128), F32),
        pltpu.VMEM((share, b), BF16),
        pltpu.SemaphoreType.DMA((1 + 2 * wl,)),
        pltpu.SemaphoreType.DMA((sems,)),
        pltpu.SemaphoreType.DMA((sems,)),
    ]
    scratch += [pltpu.VMEM((3, crow, b), BF16)] * CHUNKS
    scratch += [pltpu.VMEM((3, 2, share, b), BF16)] * (n // 2)
    return tuple(pl.pallas_call(
        functools.partial(kernel, dims),
        out_shape=(out, out),
        in_specs=[any_spec] * 3 + [smem] * 4,
        out_specs=(any_spec, any_spec),
        scratch_shapes=scratch,
        compiler_params=pltpu.CompilerParams(collective_id=0, has_side_effects=True),
        name="two_products",
    )(wavefunction, env_left, env_right, row_len, col_len, charge_shift, present))


def solution(mesh):
    n, ns = mesh.shape["mpo"], mesh.shape["sector"]
    nx, nz = (4, 8) if ns == 64 else (1, ns // 2)

    def body(wavefunction, env_left, env_right, row_len, col_len, charge_shift, present):
        dims = (n, ns, nx, nz, env_left.shape[0], wavefunction.shape[1])
        return shards(dims, wavefunction, env_left, env_right, row_len, col_len, charge_shift, present)

    in_specs = (
        P("sector", None, None),
        P("mpo", "sector", None, None),
        P("mpo", "sector", None, None),
        P("sector"),
        P("sector"),
        P("mpo"),
        P("mpo", "sector"),
    )
    out_specs = (P("sector", "mpo", None), P("sector", "mpo", None))
    return jax.shard_map(body, mesh=mesh, in_specs=in_specs, out_specs=out_specs, check_vma=False)
```

```python
import functools

import jax
import jax.numpy as jnp
from jax import lax
from jax.experimental import pallas as pl
from jax.experimental.pallas import tpu as pltpu
from jax.sharding import PartitionSpec as P

epsilon = 1e-06
MESH = pl.DeviceIdType.MESH
F32, BF16 = jnp.float32, jnp.bfloat16
CHUNKS = 4


def kernel(dims, wave, env_left, env_right, row_h, col_h, shift_h, pres_h, outs, row_len, col_len, shift, present,
           raw, rmat, rtrans, lcat, u, own, rs_send, rs_recv, sq_send, sq_y, sq_z, sq_x, sq_c, held,
           ld, ss, rs, *fields):
    n, ns, nx, nz, wl, b = dims
    h = n // 2
    share = b // n
    crow = b // CHUNKS
    v1, v2 = fields[:CHUNKS], fields[CHUNKS:]

    s = lax.axis_index("sector")
    y = lax.axis_index("mpo")
    core = lax.rem(s, 2)
    z = lax.rem(s // 2, nz)
    x = s // (2 * nz)
    near_s = s + 1 - 2 * core
    far_s = lax.rem(s + ns + 2 * core - 1, ns)
    near, far = (near_s, y), (far_s, y)

    def ypeer(k):
        return (s, lax.rem(y + n + k, n))

    def zpeer(k):
        return ((x * nz + lax.rem(z + k, nz)) * 2 + core, y)

    def xpeer(k):
        return ((lax.rem(x + k, nx) * nz + z) * 2 + core, y)

    bar = pltpu.get_barrier_semaphore()
    partners = [ypeer(k) for k in range(1, n)] + [near, far]
    partners += [zpeer(k) for k in range(1, nz)] + [xpeer(k) for k in range(1, nx)]
    for p in partners:
        pl.semaphore_signal(bar, inc=1, device_id=p, device_id_type=MESH)

    small = []
    for i, (a, t) in enumerate(((row_h, row_len), (col_h, col_len), (shift_h, shift), (pres_h, present))):
        c = pltpu.make_async_copy(a, t, ld.at[1 + 2 * wl + i])
        c.start()
        small.append(c)
    load_wave = pltpu.make_async_copy(wave.at[0], raw, ld.at[0])
    load_wave.start()
    load_r, load_l = [], []
    for w in range(wl):
        c = pltpu.make_async_copy(env_right.at[w, 0], rmat.at[w], ld.at[1 + w])
        c.start()
        load_r.append(c)
    for w in range(wl):
        c = pltpu.make_async_copy(env_left.at[w, 0], lcat.at[:, w * b:(w + 1) * b], ld.at[1 + wl + w])
        c.start()
        load_l.append(c)

    for c in small:
        c.wait()
    rl, cl = row_len[0], col_len[0]
    near_shift = 2 * core - 1
    slot, weight = [], []
    for w in range(wl):
        sh = shift[w]
        source = s - sh
        slot.append(jnp.where(sh == 0, 0, jnp.where(sh == near_shift, 1, 2)))
        ok = jnp.logical_and(source >= 0, source < ns)
        weight.append(jnp.where(ok, present[0, w], 0).astype(F32))

    sends = []
    counter = [0]
    sem_of = {}

    def sem(key):
        if key not in sem_of:
            sem_of[key] = counter[0]
            counter[0] += 1
        return sem_of[key]

    def send(src, dst, key, dev):
        i = sem(key)
        c = pltpu.make_async_remote_copy(src, dst, ss.at[i], rs.at[i], device_id=dev, device_id_type=MESH)
        c.start()
        sends.append(c)

    def arrived(dst, key):
        i = sem(key)
        pltpu.make_async_remote_copy(dst, dst, ss.at[i], rs.at[i], device_id=near, device_id_type=MESH).wait_recv()

    load_wave.wait()
    cmask = lax.broadcasted_iota(jnp.int32, (crow, b), 1) < cl
    rio = lax.broadcasted_iota(jnp.int32, (crow, b), 0)
    for c in range(CHUNKS):
        keep = jnp.logical_and(cmask, rio + c * crow < rl)
        v1[c][0] = jnp.where(keep, raw[c * crow:(c + 1) * crow, :].astype(F32), 0.0).astype(BF16)
        if c == 0:
            pl.semaphore_wait(bar, len(partners))
        send(v1[c].at[0], v1[c].at[2], ("h1f", c), far)
    for c in range(CHUNKS):
        send(v1[c].at[0], v1[c].at[1], ("h1n", c), near)

    for w in range(wl):
        load_r[w].wait()
        rtrans[w] = rmat[w].T
    for w in range(wl):
        load_l[w].wait()

    for c in range(CHUNKS):
        arrived(v1[c].at[1], ("h1n", c))
        arrived(v1[c].at[2], ("h1f", c))
        for w in range(wl):
            part = jnp.dot(v1[c][slot[w]], rtrans[w], preferred_element_type=F32)
            u[w * b + c * crow:w * b + (c + 1) * crow, :] = (part * weight[w]).astype(BF16)

    def start(k):
        return pl.multiple_of(lax.rem(y + n + k, n) * share, share)

    half = share // 2
    low, high = pl.ds(0, half), pl.ds(half, half)
    span = {"low": low, "high": high, "all": pl.ds(0, share)}

    def reduce_scatter(app, between):
        def two_blocks(k0, k1):
            lhs = jnp.concatenate([lcat[pl.ds(start(k0), share), :], lcat[pl.ds(start(k1), share), :]], axis=0)
            part = jnp.dot(lhs, u[...], preferred_element_type=F32)
            return part[:share], part[share:]

        def put(k, part, value):
            rs_send[app, k % n, span[part]] = value.astype(BF16)

        def go(k, part, hop):
            src, dst = rs_send.at[app, k % n, span[part]], rs_recv.at[app, k % n, span[part]]
            send(src, dst, ("rs", app, k, part), ypeer(hop))

        def got(k, part):
            arrived(rs_recv.at[app, k % n, span[part]], ("rs", app, k, part))
            return rs_recv[app, k % n, span[part]].astype(F32)

        p4, p3 = two_blocks(4, 3)
        put(3, "all", p3)
        put(4, "all", p4)
        go(3, "high", 1)
        go(4, "high", -2)
        go(3, "low", 1)
        go(4, "low", 2)
        m3, p1 = two_blocks(-3, 1)
        put(-3, "all", m3)
        go(-3, "low", -1)
        go(-3, "high", -1)
        put(1, "all", p1)
        go(1, "all", 1)
        m1, p2 = two_blocks(-1, 2)
        put(-1, "all", m1)
        go(-1, "all", -1)
        held[0] = p2
        m2, p0 = two_blocks(-2, 0)
        held[1] = m2
        own[...] = p0
        put(2, "high", held[0, high] + got(3, "high"))
        go(2, "high", 2)
        put(-2, "low", held[1, low] + got(-3, "low"))
        go(-2, "low", -2)
        put(2, "low", held[0, low] + got(3, "low") + got(4, "low"))
        go(2, "low", 2)
        put(-2, "high", held[1, high] + got(-3, "high") + got(4, "high"))
        go(-2, "high", -2)
        between()
        total = own[...] + got(1, "all") + got(-1, "all")
        upper = jnp.concatenate([got(-2, "low"), got(2, "high")], axis=0)
        lower = jnp.concatenate([got(2, "low"), got(-2, "high")], axis=0)
        total = total + upper + lower
        keep_r = lax.broadcasted_iota(jnp.int32, (share, b), 0) + y * share < rl
        keep_c = lax.broadcasted_iota(jnp.int32, (share, b), 1) < cl
        return jnp.where(jnp.logical_and(keep_r, keep_c), total, 0.0)

    image = reduce_scatter(0, lambda: None)

    def field(r, layer):
        if r in (0, h):
            return v2[0].at[layer, 0 if r == 0 else 1]
        return v2[abs(r)].at[layer, 0 if r > 0 else 1]

    v2[0][0, 0] = image.astype(BF16)
    square = image * image
    square = jnp.sum(square.reshape(share // 8, 8, b), axis=0)
    tile = square[:, 0:128]
    for q in range(128, b, 128):
        tile = tile + square[:, q:q + 128]
    sq_send[0] = tile

    def write_first():
        outs[0] = v2[0][0, 0]

    def hand_on(r):
        send(field(r, 0), field(r, 2), ("h2f", r), far)
        send(field(r, 0), field(r, 1), ("h2n", r), near)

    def pass_rows(r_here, layer_here, r_there, part, hop):
        src, dst = field(r_here, layer_here).at[span[part]], field(r_there, 0).at[span[part]]
        send(src, dst, ("ag", r_there, part), ypeer(hop))

    def rows_in(r, part):
        arrived(field(r, 0).at[span[part]], ("ag", r, part))

    pass_rows(0, 0, -2, "low", 2)
    pass_rows(0, 0, 2, "high", -2)
    pass_rows(0, 0, -2, "high", 2)
    pass_rows(0, 0, 2, "low", -2)
    pass_rows(0, 0, -1, "all", 1)
    pass_rows(0, 0, 1, "all", -1)
    hand_on(0)
    for k in range(1, n):
        send(sq_send.at[0], sq_y.at[k - 1], ("sqy", k), ypeer(k))
    write_first()

    rows_in(-2, "low")
    pass_rows(-2, 0, 4, "low", 2)
    pass_rows(-2, 0, -3, "low", 1)
    rows_in(2, "high")
    pass_rows(2, 0, 4, "high", -2)
    pass_rows(2, 0, 3, "high", -1)
    rows_in(-2, "high")
    pass_rows(-2, 0, -3, "high", 1)
    rows_in(2, "low")
    pass_rows(2, 0, 3, "low", -1)
    hand_on(-2)
    hand_on(2)
    rows_in(-1, "all")
    hand_on(-1)
    rows_in(1, "all")
    hand_on(1)
    rows_in(4, "low")
    rows_in(4, "high")
    hand_on(4)
    for r in (-3, 3):
        rows_in(r, "low")
        rows_in(r, "high")
        hand_on(r)

    total = sq_send[0]
    for k in range(1, n):
        arrived(sq_y.at[k - 1], ("sqy", k))
        total = total + sq_y[k - 1]
    sq_send[1] = total
    for k in range(1, nz):
        send(sq_send.at[1], sq_z.at[k - 1], ("sqz", k), zpeer(k))

    for g in (2, 1, 0, 3):
        members = (g, -g) if g else (0, h)
        for r in members:
            arrived(field(r, 1), ("h2n", r))
            arrived(field(r, 2), ("h2f", r))
        for w in range(wl):
            lhs = v2[g][slot[w]].reshape(2 * share, b)
            part = (jnp.dot(lhs, rtrans[w], preferred_element_type=F32) * weight[w]).astype(BF16)
            for i, r in enumerate(members):
                u[pl.ds(w * b + start(r), share), :] = part[i * share:(i + 1) * share]

    def norm_steps():
        total = sq_send[1]
        for k in range(1, nz):
            arrived(sq_z.at[k - 1], ("sqz", k))
            total = total + sq_z[k - 1]
        sq_send[2] = total
        for k in range(1, nx):
            send(sq_send.at[2], sq_x.at[k - 1], ("sqx", k), xpeer(k))
        for k in range(1, nx):
            arrived(sq_x.at[k - 1], ("sqx", k))
            total = total + sq_x[k - 1]
        sq_send[3] = total
        send(sq_send.at[3], sq_c, ("sqc", 0), near)
        arrived(sq_c, ("sqc", 0))
        sq_send[4] = total + sq_c[...]

    second = reduce_scatter(1, norm_steps)
    norm = jnp.sum(sq_send[4]) / (ns * b * b) + epsilon
    outs[1] = (second * (1.0 / jnp.sqrt(jnp.full((1, 1), norm, F32)))).astype(BF16)
    for c in sends:
        c.wait_send()
    assert counter[0] <= ss.shape[0]


def shards(dims, wavefunction, env_left, env_right, row_len, col_len, charge_shift, present):
    n, ns, nx, nz, wl, b = dims
    share, crow = b // n, b // CHUNKS
    any_spec = pl.BlockSpec(memory_space=pl.ANY)
    smem = pl.BlockSpec(memory_space=pltpu.SMEM)
    out = jax.ShapeDtypeStruct((1, share, b), BF16)
    sems = 2 * CHUNKS + 24 + 12 + 2 * n + (n - 1) + (nz - 1) + (nx - 1) + 1
    scratch = [
        pltpu.SMEM((1,), jnp.int32), pltpu.SMEM((1,), jnp.int32), pltpu.SMEM((wl,), jnp.int32), pltpu.SMEM((1, wl), jnp.int32),
        pltpu.VMEM((b, b), BF16),
        pltpu.VMEM((wl, b, b), BF16),
        pltpu.VMEM((wl, b, b), BF16),
        pltpu.VMEM((b, wl * b), BF16),
        pltpu.VMEM((wl * b, b), BF16),
        pltpu.VMEM((share, b), F32),
        pltpu.VMEM((2, n, share, b), BF16),
        pltpu.VMEM((2, n, share, b), BF16),
        pltpu.VMEM((5, 8, 128), F32),
        pltpu.VMEM((n - 1, 8, 128), F32),
        pltpu.VMEM((max(nz - 1, 1), 8, 128), F32),
        pltpu.VMEM((max(nx - 1, 1), 8, 128), F32),
        pltpu.VMEM((8, 128), F32),
        pltpu.VMEM((2, share, b), F32),
        pltpu.SemaphoreType.DMA((5 + 2 * wl,)),
        pltpu.SemaphoreType.DMA((sems,)),
        pltpu.SemaphoreType.DMA((sems,)),
    ]
    scratch += [pltpu.VMEM((3, crow, b), BF16)] * CHUNKS
    scratch += [pltpu.VMEM((3, 2, share, b), BF16)] * (n // 2)
    o = pl.pallas_call(
        functools.partial(kernel, dims),
        out_shape=jax.ShapeDtypeStruct((2, share, b), BF16),
        in_specs=[any_spec] * 7,
        out_specs=pl.BlockSpec(memory_space=pltpu.VMEM),
        scratch_shapes=scratch,
        compiler_params=pltpu.CompilerParams(collective_id=0, has_side_effects=True),
        name="two_products",
    )(wavefunction, env_left, env_right, row_len, col_len, charge_shift, present.T)
    return o[0:1], o[1:2]


def solution(mesh):
    n, ns = mesh.shape["mpo"], mesh.shape["sector"]
    nx, nz = (4, 8) if ns == 64 else (1, ns // 2)

    def body(wavefunction, env_left, env_right, row_len, col_len, charge_shift, present):
        dims = (n, ns, nx, nz, env_left.shape[0], wavefunction.shape[1])
        return shards(dims, wavefunction, env_left, env_right, row_len, col_len, charge_shift, present)

    in_specs = (
        P("sector", None, None),
        P("mpo", "sector", None, None),
        P("mpo", "sector", None, None),
        P("sector"),
        P("sector"),
        P("mpo"),
        P("mpo", "sector"),
    )
    out_specs = (P("sector", "mpo", None), P("sector", "mpo", None))
    return jax.shard_map(body, mesh=mesh, in_specs=in_specs, out_specs=out_specs, check_vma=False)
```

```python
import functools

import jax
import jax.numpy as jnp
from jax import lax
from jax.experimental import pallas as pl
from jax.experimental.pallas import tpu as pltpu
from jax.sharding import PartitionSpec as P

epsilon = 1e-06
MESH = pl.DeviceIdType.MESH
F32, BF16 = jnp.float32, jnp.bfloat16
CHUNKS = 4


def kernel(dims, wave, env_left, env_right, row_h, col_h, shift_h, pres_h, outs, row_len, col_len, shift, present,
           raw, rmat, rtrans, lcat, u, own, rs_send, rs_recv, sq_send, sq_y, sq_z, sq_x, sq_c, held,
           ld, ss, rs, *fields):
    n, ns, nx, nz, wl, b = dims
    h = n // 2
    share = b // n
    crow = b // CHUNKS
    v1, v2 = fields[:CHUNKS], fields[CHUNKS:]

    s = lax.axis_index("sector")
    y = lax.axis_index("mpo")
    core = lax.rem(s, 2)
    z = lax.rem(s // 2, nz)
    x = s // (2 * nz)
    near_s = s + 1 - 2 * core
    far_s = lax.rem(s + ns + 2 * core - 1, ns)
    near, far = (near_s, y), (far_s, y)

    def ypeer(k):
        return (s, lax.rem(y + n + k, n))

    def zpeer(k):
        return ((x * nz + lax.rem(z + k, nz)) * 2 + core, y)

    def xpeer(k):
        return ((lax.rem(x + k, nx) * nz + z) * 2 + core, y)

    bar = pltpu.get_barrier_semaphore()
    partners = [ypeer(k) for k in range(1, n)] + [near, far]
    partners += [zpeer(k) for k in range(1, nz)] + [xpeer(k) for k in range(1, nx)]
    for p in partners:
        pl.semaphore_signal(bar, inc=1, device_id=p, device_id_type=MESH)

    small = []
    for i, (a, t) in enumerate(((row_h, row_len), (col_h, col_len), (shift_h, shift), (pres_h, present))):
        c = pltpu.make_async_copy(a, t, ld.at[1 + 2 * wl + i])
        c.start()
        small.append(c)
    load_wave = pltpu.make_async_copy(wave.at[0], raw, ld.at[0])
    load_wave.start()
    load_r, load_l = [], []
    for w in range(wl):
        c = pltpu.make_async_copy(env_right.at[w, 0], rmat.at[w], ld.at[1 + w])
        c.start()
        load_r.append(c)
    for w in range(wl):
        c = pltpu.make_async_copy(env_left.at[w, 0], lcat.at[:, w * b:(w + 1) * b], ld.at[1 + wl + w])
        c.start()
        load_l.append(c)

    for c in small:
        c.wait()
    rl, cl = row_len[0], col_len[0]
    near_shift = 2 * core - 1
    slot, weight = [], []
    for w in range(wl):
        sh = shift[w]
        source = s - sh
        slot.append(jnp.where(sh == 0, 0, jnp.where(sh == near_shift, 1, 2)))
        ok = jnp.logical_and(source >= 0, source < ns)
        weight.append(jnp.where(ok, present[0, w], 0).astype(F32))

    sends = []
    counter = [0]
    sem_of = {}

    def sem(key):
        if key not in sem_of:
            sem_of[key] = counter[0]
            counter[0] += 1
        return sem_of[key]

    def send(src, dst, key, dev):
        i = sem(key)
        c = pltpu.make_async_remote_copy(src, dst, ss.at[i], rs.at[i], device_id=dev, device_id_type=MESH)
        c.start()
        sends.append(c)

    def arrived(dst, key):
        i = sem(key)
        pltpu.make_async_remote_copy(dst, dst, ss.at[i], rs.at[i], device_id=near, device_id_type=MESH).wait_recv()

    load_wave.wait()
    cmask = lax.broadcasted_iota(jnp.int32, (crow, b), 1) < cl
    rio = lax.broadcasted_iota(jnp.int32, (crow, b), 0)
    for c in range(CHUNKS):
        keep = jnp.logical_and(cmask, rio + c * crow < rl)
        v1[c][0] = jnp.where(keep, raw[c * crow:(c + 1) * crow, :].astype(F32), 0.0).astype(BF16)
        if c == 0:
            pl.semaphore_wait(bar, len(partners))
        send(v1[c].at[0], v1[c].at[2], ("h1f", c), far)
    for c in range(CHUNKS):
        send(v1[c].at[0], v1[c].at[1], ("h1n", c), near)

    for w in range(wl):
        load_r[w].wait()
        rtrans[w] = rmat[w].T
    for w in range(wl):
        load_l[w].wait()

    for c in range(CHUNKS):
        arrived(v1[c].at[1], ("h1n", c))
        arrived(v1[c].at[2], ("h1f", c))
        for w in range(wl):
            part = jnp.dot(v1[c][slot[w]], rtrans[w], preferred_element_type=F32)
            u[w * b + c * crow:w * b + (c + 1) * crow, :] = (part * weight[w]).astype(BF16)

    def start(k):
        return pl.multiple_of(lax.rem(y + n + k, n) * share, share)

    half = share // 2
    low, high = pl.ds(0, half), pl.ds(half, half)
    span = {"low": low, "high": high, "all": pl.ds(0, share)}

    def reduce_scatter(app, midway=None, between=None):
        def two_blocks(k0, k1):
            lhs = jnp.concatenate([lcat[pl.ds(start(k0), share), :], lcat[pl.ds(start(k1), share), :]], axis=0)
            part = jnp.dot(lhs, u[...], preferred_element_type=F32)
            return part[:share], part[share:]

        def put(k, part, value):
            rs_send[app, k % n, span[part]] = value.astype(BF16)

        def go(k, part, hop):
            src, dst = rs_send.at[app, k % n, span[part]], rs_recv.at[app, k % n, span[part]]
            send(src, dst, ("rs", app, k, part), ypeer(hop))

        def got(k, part):
            arrived(rs_recv.at[app, k % n, span[part]], ("rs", app, k, part))
            return rs_recv[app, k % n, span[part]].astype(F32)

        p4, p3 = two_blocks(4, 3)
        put(3, "all", p3)
        put(4, "all", p4)
        go(3, "high", 1)
        go(4, "high", -2)
        go(3, "low", 1)
        go(4, "low", 2)
        m3, p1 = two_blocks(-3, 1)
        put(-3, "all", m3)
        go(-3, "low", -1)
        go(-3, "high", -1)
        put(1, "all", p1)
        go(1, "all", 1)
        m1, p2 = two_blocks(-1, 2)
        put(-1, "all", m1)
        go(-1, "all", -1)
        held[0] = p2
        m2, p0 = two_blocks(-2, 0)
        held[1] = m2
        own[...] = p0
        put(2, "high", held[0, high] + got(3, "high"))
        go(2, "high", 2)
        put(-2, "low", held[1, low] + got(-3, "low"))
        go(-2, "low", -2)
        if midway is not None:
            midway()
        put(2, "low", held[0, low] + got(3, "low") + got(4, "low"))
        go(2, "low", 2)
        put(-2, "high", held[1, high] + got(-3, "high") + got(4, "high"))
        go(-2, "high", -2)
        if between is not None:
            between()
        total = own[...] + got(1, "all") + got(-1, "all")
        upper = jnp.concatenate([got(-2, "low"), got(2, "high")], axis=0)
        lower = jnp.concatenate([got(2, "low"), got(-2, "high")], axis=0)
        total = total + upper + lower
        keep_r = lax.broadcasted_iota(jnp.int32, (share, b), 0) + y * share < rl
        keep_c = lax.broadcasted_iota(jnp.int32, (share, b), 1) < cl
        return jnp.where(jnp.logical_and(keep_r, keep_c), total, 0.0)

    image = reduce_scatter(0)

    def field(r, layer):
        if r in (0, h):
            return v2[0].at[layer, 0 if r == 0 else 1]
        return v2[abs(r)].at[layer, 0 if r > 0 else 1]

    v2[0][0, 0] = image.astype(BF16)
    square = image * image
    square = jnp.sum(square.reshape(share // 8, 8, b), axis=0)
    tile = square[:, 0:128]
    for q in range(128, b, 128):
        tile = tile + square[:, q:q + 128]
    sq_send[0] = tile

    def write_first():
        outs[0] = v2[0][0, 0]

    def hand_on(r):
        send(field(r, 0), field(r, 2), ("h2f", r), far)
        send(field(r, 0), field(r, 1), ("h2n", r), near)

    def pass_rows(r_here, layer_here, r_there, part, hop):
        src, dst = field(r_here, layer_here).at[span[part]], field(r_there, 0).at[span[part]]
        send(src, dst, ("ag", r_there, part), ypeer(hop))

    def rows_in(r, part):
        arrived(field(r, 0).at[span[part]], ("ag", r, part))

    pass_rows(0, 0, -2, "low", 2)
    pass_rows(0, 0, 2, "high", -2)
    pass_rows(0, 0, -2, "high", 2)
    pass_rows(0, 0, 2, "low", -2)
    pass_rows(0, 0, -1, "all", 1)
    pass_rows(0, 0, 1, "all", -1)
    hand_on(0)
    for k in range(1, n):
        send(sq_send.at[0], sq_y.at[k - 1], ("sqy", k), ypeer(k))
    write_first()

    rows_in(-2, "low")
    pass_rows(-2, 0, 4, "low", 2)
    pass_rows(-2, 0, -3, "low", 1)
    rows_in(2, "high")
    pass_rows(2, 0, 4, "high", -2)
    pass_rows(2, 0, 3, "high", -1)
    rows_in(-2, "high")
    pass_rows(-2, 0, -3, "high", 1)
    rows_in(2, "low")
    pass_rows(2, 0, 3, "low", -1)
    hand_on(-2)
    hand_on(2)
    rows_in(-1, "all")
    hand_on(-1)
    rows_in(1, "all")
    hand_on(1)
    rows_in(4, "low")
    rows_in(4, "high")
    hand_on(4)
    for r in (-3, 3):
        rows_in(r, "low")
        rows_in(r, "high")
        hand_on(r)

    total = sq_send[0]
    for k in range(1, n):
        arrived(sq_y.at[k - 1], ("sqy", k))
        total = total + sq_y[k - 1]
    sq_send[1] = total
    for k in range(1, nz):
        send(sq_send.at[1], sq_z.at[k - 1], ("sqz", k), zpeer(k))

    for g in (2, 1, 0, 3):
        members = (g, -g) if g else (0, h)
        for r in members:
            arrived(field(r, 1), ("h2n", r))
            arrived(field(r, 2), ("h2f", r))
        for w in range(wl):
            lhs = v2[g][slot[w]].reshape(2 * share, b)
            part = (jnp.dot(lhs, rtrans[w], preferred_element_type=F32) * weight[w]).astype(BF16)
            for i, r in enumerate(members):
                u[pl.ds(w * b + start(r), share), :] = part[i * share:(i + 1) * share]

    for k in range(1, nz):
        arrived(sq_z.at[k - 1], ("sqz", k))
        total = total + sq_z[k - 1]
    sq_send[2] = total
    for k in range(1, nx):
        send(sq_send.at[2], sq_x.at[k - 1], ("sqx", k), xpeer(k))

    def collect_x():
        total = sq_send[2]
        for k in range(1, nx):
            arrived(sq_x.at[k - 1], ("sqx", k))
            total = total + sq_x[k - 1]
        sq_send[3] = total
        send(sq_send.at[3], sq_c, ("sqc", 0), near)

    def collect_core():
        arrived(sq_c, ("sqc", 0))
        norm = jnp.sum(sq_send[3] + sq_c[...]) / (ns * b * b) + epsilon
        sq_send[4] = 1.0 / jnp.sqrt(jnp.full((8, 128), norm, F32))

    second = reduce_scatter(1, collect_x, collect_core)
    outs[1] = (second * sq_send[4, 0:1, 0:1]).astype(BF16)
    for c in sends:
        c.wait_send()
    assert counter[0] <= ss.shape[0]


def shards(dims, wavefunction, env_left, env_right, row_len, col_len, charge_shift, present):
    n, ns, nx, nz, wl, b = dims
    share, crow = b // n, b // CHUNKS
    any_spec = pl.BlockSpec(memory_space=pl.ANY)
    smem = pl.BlockSpec(memory_space=pltpu.SMEM)
    out = jax.ShapeDtypeStruct((1, share, b), BF16)
    sems = 2 * CHUNKS + 24 + 12 + 2 * n + (n - 1) + (nz - 1) + (nx - 1) + 1
    scratch = [
        pltpu.SMEM((1,), jnp.int32), pltpu.SMEM((1,), jnp.int32), pltpu.SMEM((wl,), jnp.int32), pltpu.SMEM((1, wl), jnp.int32),
        pltpu.VMEM((b, b), BF16),
        pltpu.VMEM((wl, b, b), BF16),
        pltpu.VMEM((wl, b, b), BF16),
        pltpu.VMEM((b, wl * b), BF16),
        pltpu.VMEM((wl * b, b), BF16),
        pltpu.VMEM((share, b), F32),
        pltpu.VMEM((2, n, share, b), BF16),
        pltpu.VMEM((2, n, share, b), BF16),
        pltpu.VMEM((5, 8, 128), F32),
        pltpu.VMEM((n - 1, 8, 128), F32),
        pltpu.VMEM((max(nz - 1, 1), 8, 128), F32),
        pltpu.VMEM((max(nx - 1, 1), 8, 128), F32),
        pltpu.VMEM((8, 128), F32),
        pltpu.VMEM((2, share, b), F32),
        pltpu.SemaphoreType.DMA((5 + 2 * wl,)),
        pltpu.SemaphoreType.DMA((sems,)),
        pltpu.SemaphoreType.DMA((sems,)),
    ]
    scratch += [pltpu.VMEM((3, crow, b), BF16)] * CHUNKS
    scratch += [pltpu.VMEM((3, 2, share, b), BF16)] * (n // 2)
    o = pl.pallas_call(
        functools.partial(kernel, dims),
        out_shape=jax.ShapeDtypeStruct((2, share, b), BF16),
        in_specs=[any_spec] * 7,
        out_specs=pl.BlockSpec(memory_space=pltpu.VMEM),
        scratch_shapes=scratch,
        compiler_params=pltpu.CompilerParams(collective_id=0, has_side_effects=True),
        name="two_products",
    )(wavefunction, env_left, env_right, row_len, col_len, charge_shift, present.T)
    return o[0:1], o[1:2]


def solution(mesh):
    n, ns = mesh.shape["mpo"], mesh.shape["sector"]
    nx, nz = (4, 8) if ns == 64 else (1, ns // 2)

    def body(wavefunction, env_left, env_right, row_len, col_len, charge_shift, present):
        dims = (n, ns, nx, nz, env_left.shape[0], wavefunction.shape[1])
        return shards(dims, wavefunction, env_left, env_right, row_len, col_len, charge_shift, present)

    in_specs = (
        P("sector", None, None),
        P("mpo", "sector", None, None),
        P("mpo", "sector", None, None),
        P("sector"),
        P("sector"),
        P("mpo"),
        P("mpo", "sector"),
    )
    out_specs = (P("sector", "mpo", None), P("sector", "mpo", None))
    return jax.shard_map(body, mesh=mesh, in_specs=in_specs, out_specs=out_specs, check_vma=False)
```

```python
import functools

import jax
import jax.numpy as jnp
from jax import lax
from jax.experimental import pallas as pl
from jax.experimental.pallas import tpu as pltpu
from jax.sharding import PartitionSpec as P

epsilon = 1e-06
MESH = pl.DeviceIdType.MESH
F32, BF16 = jnp.float32, jnp.bfloat16
CHUNKS = 4


def kernel(dims, wave, env_left, env_right, row_h, col_h, shift_h, pres_h, outs, row_len, col_len, shift, present,
           raw, rmat, rtrans, lcat, u, own, rs_send, rs_recv, sq_send, sq_y, sq_z, sq_x, sq_c, held,
           ld, ss, rs, *fields):
    n, ns, nx, nz, wl, b = dims
    h = n // 2
    share = b // n
    crow = b // CHUNKS
    v1, v2 = fields[:CHUNKS], fields[CHUNKS:]

    s = lax.axis_index("sector")
    y = lax.axis_index("mpo")
    core = lax.rem(s, 2)
    z = lax.rem(s // 2, nz)
    x = s // (2 * nz)
    near_s = s + 1 - 2 * core
    far_s = lax.rem(s + ns + 2 * core - 1, ns)
    near, far = (near_s, y), (far_s, y)

    def ypeer(k):
        return (s, lax.rem(y + n + k, n))

    def zpeer(k):
        return ((x * nz + lax.rem(z + k, nz)) * 2 + core, y)

    def xpeer(k):
        return ((lax.rem(x + k, nx) * nz + z) * 2 + core, y)

    bar = pltpu.get_barrier_semaphore()
    partners = [ypeer(k) for k in range(1, n)] + [near, far]
    partners += [zpeer(k) for k in range(1, nz)] + [xpeer(k) for k in range(1, nx)]
    for p in partners:
        pl.semaphore_signal(bar, inc=1, device_id=p, device_id_type=MESH)

    small = []
    for i, (a, t) in enumerate(((row_h, row_len), (col_h, col_len), (shift_h, shift), (pres_h, present))):
        c = pltpu.make_async_copy(a, t, ld.at[1 + 2 * wl + i])
        c.start()
        small.append(c)
    load_wave = pltpu.make_async_copy(wave.at[0], raw, ld.at[0])
    load_wave.start()
    load_r, load_l = [], []
    for w in range(wl):
        c = pltpu.make_async_copy(env_right.at[w, 0], rmat.at[w], ld.at[1 + w])
        c.start()
        load_r.append(c)
    for w in range(wl):
        c = pltpu.make_async_copy(env_left.at[w, 0], lcat.at[:, w * b:(w + 1) * b], ld.at[1 + wl + w])
        c.start()
        load_l.append(c)

    for c in small:
        c.wait()
    rl, cl = row_len[0], col_len[0]
    near_shift = 2 * core - 1
    slot, weight = [], []
    for w in range(wl):
        sh = shift[w]
        source = s - sh
        slot.append(jnp.where(sh == 0, 0, jnp.where(sh == near_shift, 1, 2)))
        ok = jnp.logical_and(source >= 0, source < ns)
        weight.append(jnp.where(ok, present[0, w], 0).astype(F32))

    sends = []
    counter = [0]
    sem_of = {}

    def sem(key):
        if key not in sem_of:
            sem_of[key] = counter[0]
            counter[0] += 1
        return sem_of[key]

    has_far = jnp.logical_and(s + 2 * core > 0, s + 2 * core < ns + 1)

    def send(src, dst, key, dev):
        i = sem(key)
        c = pltpu.make_async_remote_copy(src, dst, ss.at[i], rs.at[i], device_id=dev, device_id_type=MESH)
        if dev is far:
            pl.when(has_far)(c.start)
        else:
            c.start()
        sends.append((c, dev is far))

    def arrived(dst, key, from_far=False):
        i = sem(key)
        c = pltpu.make_async_remote_copy(dst, dst, ss.at[i], rs.at[i], device_id=near, device_id_type=MESH)
        if from_far:
            pl.when(has_far)(c.wait_recv)
        else:
            c.wait_recv()

    @pl.when(jnp.logical_not(has_far))
    def _():
        for f in fields:
            f[2] = jnp.zeros(f.shape[1:], BF16)

    load_wave.wait()
    cmask = lax.broadcasted_iota(jnp.int32, (crow, b), 1) < cl
    rio = lax.broadcasted_iota(jnp.int32, (crow, b), 0)
    for c in range(CHUNKS):
        keep = jnp.logical_and(cmask, rio + c * crow < rl)
        v1[c][0] = jnp.where(keep, raw[c * crow:(c + 1) * crow, :].astype(F32), 0.0).astype(BF16)
        if c == 0:
            pl.semaphore_wait(bar, len(partners))
        send(v1[c].at[0], v1[c].at[2], ("h1f", c), far)
    for c in range(CHUNKS):
        send(v1[c].at[0], v1[c].at[1], ("h1n", c), near)

    for w in range(wl):
        load_r[w].wait()
        rtrans[w] = rmat[w].T
    for w in range(wl):
        load_l[w].wait()

    for c in range(CHUNKS):
        arrived(v1[c].at[1], ("h1n", c))
        arrived(v1[c].at[2], ("h1f", c), True)
        for w in range(wl):
            part = jnp.dot(v1[c][slot[w]], rtrans[w], preferred_element_type=F32)
            u[w * b + c * crow:w * b + (c + 1) * crow, :] = (part * weight[w]).astype(BF16)

    def start(k):
        return pl.multiple_of(lax.rem(y + n + k, n) * share, share)

    half = share // 2
    low, high = pl.ds(0, half), pl.ds(half, half)
    span = {"low": low, "high": high, "all": pl.ds(0, share)}

    def reduce_scatter(app, midway=None, between=None):
        def two_blocks(k0, k1):
            lhs = jnp.concatenate([lcat[pl.ds(start(k0), share), :], lcat[pl.ds(start(k1), share), :]], axis=0)
            part = jnp.dot(lhs, u[...], preferred_element_type=F32)
            return part[:share], part[share:]

        def put(k, part, value):
            rs_send[app, k % n, span[part]] = value.astype(BF16)

        def go(k, part, hop):
            src, dst = rs_send.at[app, k % n, span[part]], rs_recv.at[app, k % n, span[part]]
            send(src, dst, ("rs", app, k, part), ypeer(hop))

        def got(k, part):
            arrived(rs_recv.at[app, k % n, span[part]], ("rs", app, k, part))
            return rs_recv[app, k % n, span[part]].astype(F32)

        p4, p3 = two_blocks(4, 3)
        put(3, "all", p3)
        put(4, "all", p4)
        go(3, "high", 1)
        go(4, "high", -2)
        go(3, "low", 1)
        go(4, "low", 2)
        m3, p1 = two_blocks(-3, 1)
        put(-3, "all", m3)
        go(-3, "low", -1)
        go(-3, "high", -1)
        put(1, "all", p1)
        go(1, "all", 1)
        m1, p2 = two_blocks(-1, 2)
        put(-1, "all", m1)
        go(-1, "all", -1)
        held[0] = p2
        m2, p0 = two_blocks(-2, 0)
        held[1] = m2
        own[...] = p0
        put(2, "high", held[0, high] + got(3, "high"))
        go(2, "high", 2)
        put(-2, "low", held[1, low] + got(-3, "low"))
        go(-2, "low", -2)
        if midway is not None:
            midway()
        put(2, "low", held[0, low] + got(3, "low") + got(4, "low"))
        go(2, "low", 2)
        put(-2, "high", held[1, high] + got(-3, "high") + got(4, "high"))
        go(-2, "high", -2)
        if between is not None:
            between()
        total = own[...] + got(1, "all") + got(-1, "all")
        upper = jnp.concatenate([got(-2, "low"), got(2, "high")], axis=0)
        lower = jnp.concatenate([got(2, "low"), got(-2, "high")], axis=0)
        total = total + upper + lower
        keep_r = lax.broadcasted_iota(jnp.int32, (share, b), 0) + y * share < rl
        keep_c = lax.broadcasted_iota(jnp.int32, (share, b), 1) < cl
        return jnp.where(jnp.logical_and(keep_r, keep_c), total, 0.0)

    image = reduce_scatter(0)

    def field(r, layer):
        if r in (0, h):
            return v2[0].at[layer, 0 if r == 0 else 1]
        return v2[abs(r)].at[layer, 0 if r > 0 else 1]

    v2[0][0, 0] = image.astype(BF16)
    square = image * image
    square = jnp.sum(square.reshape(share // 8, 8, b), axis=0)
    tile = square[:, 0:128]
    for q in range(128, b, 128):
        tile = tile + square[:, q:q + 128]
    sq_send[0] = tile

    def write_first():
        outs[0] = v2[0][0, 0]

    def hand_on(r):
        send(field(r, 0), field(r, 2), ("h2f", r), far)
        send(field(r, 0), field(r, 1), ("h2n", r), near)

    def pass_rows(r_here, layer_here, r_there, part, hop):
        src, dst = field(r_here, layer_here).at[span[part]], field(r_there, 0).at[span[part]]
        send(src, dst, ("ag", r_there, part), ypeer(hop))

    def rows_in(r, part):
        arrived(field(r, 0).at[span[part]], ("ag", r, part))

    pass_rows(0, 0, -2, "low", 2)
    pass_rows(0, 0, 2, "high", -2)
    pass_rows(0, 0, -2, "high", 2)
    pass_rows(0, 0, 2, "low", -2)
    pass_rows(0, 0, -1, "all", 1)
    pass_rows(0, 0, 1, "all", -1)
    hand_on(0)
    for k in range(1, n):
        send(sq_send.at[0], sq_y.at[k - 1], ("sqy", k), ypeer(k))
    write_first()

    rows_in(-2, "low")
    pass_rows(-2, 0, 4, "low", 2)
    pass_rows(-2, 0, -3, "low", 1)
    rows_in(2, "high")
    pass_rows(2, 0, 4, "high", -2)
    pass_rows(2, 0, 3, "high", -1)
    rows_in(-2, "high")
    pass_rows(-2, 0, -3, "high", 1)
    rows_in(2, "low")
    pass_rows(2, 0, 3, "low", -1)
    hand_on(-2)
    hand_on(2)
    rows_in(-1, "all")
    hand_on(-1)
    rows_in(1, "all")
    hand_on(1)
    rows_in(4, "low")
    rows_in(4, "high")
    hand_on(4)
    for r in (-3, 3):
        rows_in(r, "low")
        rows_in(r, "high")
        hand_on(r)

    total = sq_send[0]
    for k in range(1, n):
        arrived(sq_y.at[k - 1], ("sqy", k))
        total = total + sq_y[k - 1]
    sq_send[1] = total
    for k in range(1, nz):
        send(sq_send.at[1], sq_z.at[k - 1], ("sqz", k), zpeer(k))

    for g in (2, 1, 0, 3):
        members = (g, -g) if g else (0, h)
        for r in members:
            arrived(field(r, 1), ("h2n", r))
            arrived(field(r, 2), ("h2f", r), True)
        for w in range(wl):
            lhs = v2[g][slot[w]].reshape(2 * share, b)
            part = (jnp.dot(lhs, rtrans[w], preferred_element_type=F32) * weight[w]).astype(BF16)
            for i, r in enumerate(members):
                u[pl.ds(w * b + start(r), share), :] = part[i * share:(i + 1) * share]

    for k in range(1, nz):
        arrived(sq_z.at[k - 1], ("sqz", k))
        total = total + sq_z[k - 1]
    sq_send[2] = total
    for k in range(1, nx):
        send(sq_send.at[2], sq_x.at[k - 1], ("sqx", k), xpeer(k))

    def collect_x():
        total = sq_send[2]
        for k in range(1, nx):
            arrived(sq_x.at[k - 1], ("sqx", k))
            total = total + sq_x[k - 1]
        sq_send[3] = total
        send(sq_send.at[3], sq_c, ("sqc", 0), near)

    def collect_core():
        arrived(sq_c, ("sqc", 0))
        norm = jnp.sum(sq_send[3] + sq_c[...]) / (ns * b * b) + epsilon
        sq_send[4] = 1.0 / jnp.sqrt(jnp.full((8, 128), norm, F32))

    second = reduce_scatter(1, collect_x, collect_core)
    outs[1] = (second * sq_send[4, 0:1, 0:1]).astype(BF16)
    for c, to_far in sends:
        if to_far:
            pl.when(has_far)(c.wait_send)
        else:
            c.wait_send()
    assert counter[0] <= ss.shape[0]


def shards(dims, wavefunction, env_left, env_right, row_len, col_len, charge_shift, present):
    n, ns, nx, nz, wl, b = dims
    share, crow = b // n, b // CHUNKS
    any_spec = pl.BlockSpec(memory_space=pl.ANY)
    smem = pl.BlockSpec(memory_space=pltpu.SMEM)
    out = jax.ShapeDtypeStruct((1, share, b), BF16)
    sems = 2 * CHUNKS + 24 + 12 + 2 * n + (n - 1) + (nz - 1) + (nx - 1) + 1
    scratch = [
        pltpu.SMEM((1,), jnp.int32), pltpu.SMEM((1,), jnp.int32), pltpu.SMEM((wl,), jnp.int32), pltpu.SMEM((1, wl), jnp.int32),
        pltpu.VMEM((b, b), BF16),
        pltpu.VMEM((wl, b, b), BF16),
        pltpu.VMEM((wl, b, b), BF16),
        pltpu.VMEM((b, wl * b), BF16),
        pltpu.VMEM((wl * b, b), BF16),
        pltpu.VMEM((share, b), F32),
        pltpu.VMEM((2, n, share, b), BF16),
        pltpu.VMEM((2, n, share, b), BF16),
        pltpu.VMEM((5, 8, 128), F32),
        pltpu.VMEM((n - 1, 8, 128), F32),
        pltpu.VMEM((max(nz - 1, 1), 8, 128), F32),
        pltpu.VMEM((max(nx - 1, 1), 8, 128), F32),
        pltpu.VMEM((8, 128), F32),
        pltpu.VMEM((2, share, b), F32),
        pltpu.SemaphoreType.DMA((5 + 2 * wl,)),
        pltpu.SemaphoreType.DMA((sems,)),
        pltpu.SemaphoreType.DMA((sems,)),
    ]
    scratch += [pltpu.VMEM((3, crow, b), BF16)] * CHUNKS
    scratch += [pltpu.VMEM((3, 2, share, b), BF16)] * (n // 2)
    o = pl.pallas_call(
        functools.partial(kernel, dims),
        out_shape=jax.ShapeDtypeStruct((2, share, b), BF16),
        in_specs=[any_spec] * 7,
        out_specs=pl.BlockSpec(memory_space=pltpu.VMEM),
        scratch_shapes=scratch,
        compiler_params=pltpu.CompilerParams(collective_id=0, has_side_effects=True),
        name="two_products",
    )(wavefunction, env_left, env_right, row_len, col_len, charge_shift, present.T)
    return o[0:1], o[1:2]


def solution(mesh):
    n, ns = mesh.shape["mpo"], mesh.shape["sector"]
    nx, nz = (4, 8) if ns == 64 else (1, ns // 2)

    def body(wavefunction, env_left, env_right, row_len, col_len, charge_shift, present):
        dims = (n, ns, nx, nz, env_left.shape[0], wavefunction.shape[1])
        return shards(dims, wavefunction, env_left, env_right, row_len, col_len, charge_shift, present)

    in_specs = (
        P("sector", None, None),
        P("mpo", "sector", None, None),
        P("mpo", "sector", None, None),
        P("sector"),
        P("sector"),
        P("mpo"),
        P("mpo", "sector"),
    )
    out_specs = (P("sector", "mpo", None), P("sector", "mpo", None))
    return jax.shard_map(body, mesh=mesh, in_specs=in_specs, out_specs=out_specs, check_vma=False)
```
